32 devices in a mesh: dp: 2 (over y), seq: 16 (over z, x, core).
Axes of the slice: x: 2, y: 2, z: 4, core: 2. Of those that a mesh axis runs over, the one named last changes fastest.
Arguments:
- tokens: bfloat16 [2, 4096, 768], P('dp', 'seq'), may hold values from -9 to 9
- valid_mask: int32 [2, 4096], P('dp', 'seq'), may hold values from 0 to 1, as said below
- w_query: bfloat16 [768, 768], replicated, may hold values from -1 to 1
- w_key: bfloat16 [768, 768], replicated, may hold values from -1 to 1
- w_value: bfloat16 [768, 768], replicated, may hold values from -0.21875 to 0.21875
- w_out: bfloat16 [768, 768], replicated, may hold values from -0.21875 to 0.21875
- result_grad: bfloat16 [2, 4096, 768], P('dp', 'seq'), may hold values from -6 to 6
Outputs:
- result: bfloat16 [2, 4096, 768], P('dp', 'seq')
- token_grads: bfloat16 [2, 4096, 768], P('dp', 'seq')
- weight_grads: float32 [4, 768, 768], P(None, 'seq')
The draws below stay inside these ranges and needn't reach their ends.
Inputs may be any that keep to these rules, and one draw needn't show every extreme that they name: `valid_mask`: in every sequence the positions whose index modulo 64 is below 8 are 1.
All inputs are finite; a program needn't handle non-finite values.
Results may differ from the reference program's by a relative error of at most 0.0095.
Values may be sent and summed in bfloat16 or wider, within the bound.
A program may use at most 128 MiB of HBM per device.

```python
import math
import jax
import jax.numpy as jnp
from jax import lax

D = 768
HEADS = 16
HEAD_DIM = 48
GROUPS = 4
LEN = 4096
SEQS = 2


def draw_tokens(key, part):
    first_key = jax.random.fold_in(key, 0)
    return jax.random.truncated_normal(first_key, -6.0, 6.0, (SEQS, LEN, D), jnp.float32).astype(jnp.bfloat16)


def shared_query(key):
    return jax.random.truncated_normal(jax.random.fold_in(key, 11), -6.0, 6.0, (D, D), jnp.float32) / math.sqrt(D)


def draw_w_query(key, part):
    return shared_query(key).astype(jnp.bfloat16)


def draw_w_key(key, part):
    fresh = jax.random.truncated_normal(jax.random.fold_in(key, 12), -6.0, 6.0, (D, D), jnp.float32) / math.sqrt(D)
    return fresh.astype(jnp.bfloat16)


def draw_valid_mask(key, part):
    coins = jax.random.randint(jax.random.fold_in(key, 13), (SEQS, LEN), 0, 8)
    forced = (jnp.arange(LEN) % 64 < 8)[None, :]
    return jnp.where(forced, 1, jnp.where(coins > 0, 1, 0)).astype(jnp.int32)


def level_of(own_key, extent, cuts, low, largest):
    def one(axis_at, shards_of):
        draws = jax.random.uniform(jax.random.fold_in(jax.random.fold_in(own_key, 6), axis_at), (shards_of,), jnp.float32, low / len(cuts), largest / len(cuts))
        return jnp.repeat(jnp.exp(draws), extent[axis_at] // shards_of).reshape((-1,) + (1,) * (len(extent) - axis_at - 1))

    gain = one(*cuts[0])
    for cut in cuts[1:]:
        gain = gain * one(*cut)
    return gain


def scatter_about(rng, extent, deviation, reach, shards=(), kind=jnp.bfloat16):
    array = jax.random.normal(rng, extent, jnp.float32) * deviation
    if len(shards) > 0:
        array = level_of(rng, extent, shards, -0.22, 0.18) * array
    return jnp.clip(array, min=-reach, max=reach).astype(kind)


def setup_inputs(seed: int = 0) -> dict:
    arg_keys = jax.random.split(jax.random.key(seed), 8)
    return {
        "tokens": draw_tokens(jax.random.fold_in(arg_keys[7], 71), 0),
        "valid_mask": draw_valid_mask(jax.random.fold_in(arg_keys[7], 71), 0),
        "w_query": draw_w_query(jax.random.fold_in(arg_keys[7], 71), 0),
        "w_key": draw_w_key(jax.random.fold_in(arg_keys[7], 71), 0),
        "w_value": scatter_about(arg_keys[4], (D, D), D ** -0.5, 0.21875),
        "w_out": scatter_about(arg_keys[5], (D, D), D ** -0.5, 0.21875),
        "result_grad": scatter_about(arg_keys[6], (SEQS, LEN, D), 1.0, 6.0, ((0, 2), (1, 16))),
    }


def select_rows(block, dilation, offset):
    shaped = block.reshape((block.shape[0] // dilation, dilation) + block.shape[1:])
    return shaped[:, offset]

def place_rows(chosen, dilation, offset, length):
    holder = jnp.zeros((length // dilation, dilation) + chosen.shape[1:], chosen.dtype)
    return holder.at[:, offset].set(chosen).reshape((length,) + chosen.shape[1:])

def one_sequence(inputs, w_query, w_key, w_value, w_out):
    tokens, valid_mask, result_grad = inputs
    length = tokens.shape[0]
    per_group = HEADS // GROUPS
    score_scale = 1.0 / math.sqrt(HEAD_DIM)
    queries = jnp.dot(tokens, w_query, preferred_element_type=jnp.float32).astype(jnp.bfloat16).reshape(length, HEADS, HEAD_DIM)
    keys_local = jnp.dot(tokens, w_key, preferred_element_type=jnp.float32).astype(jnp.bfloat16).reshape(length, HEADS, HEAD_DIM)
    values_local = jnp.dot(tokens, w_value, preferred_element_type=jnp.float32).astype(jnp.bfloat16).reshape(length, HEADS, HEAD_DIM)
    attn_grad = jnp.dot(result_grad, w_out.T, preferred_element_type=jnp.float32).astype(jnp.bfloat16).reshape(length, HEADS, HEAD_DIM)
    head_outs = []
    query_grads = []
    key_grads = []
    value_grads = []
    for group_id in range(GROUPS):
        dilation = 2 ** group_id
        segment = LEN * dilation // 2 ** (GROUPS - 1)
        seg_count = length // segment
        row_count = segment // dilation
        for head_in in range(per_group):
            head_id = group_id * per_group + head_in
            offset = head_in % dilation

            def take_head(block):
                return select_rows(block[:, head_id], dilation, offset).reshape(seg_count, row_count, HEAD_DIM).astype(jnp.float32)

            def spread(chosen):
                return place_rows(chosen.reshape(length // dilation, HEAD_DIM), dilation, offset, length)
            query_part = take_head(queries)
            key_part = take_head(keys_local)
            value_part = take_head(values_local)
            grad_part = take_head(attn_grad)
            key_flags = select_rows(valid_mask, dilation, offset).reshape(seg_count, row_count)
            scores = jnp.einsum('sqe,ske->sqk', query_part, key_part) * score_scale
            scores = jnp.where(key_flags[:, None, :] == 1, scores, -jnp.inf)
            row_max = lax.optimization_barrier(jnp.max(scores, axis=-1, keepdims=True))
            log_total = row_max + jnp.log(lax.optimization_barrier(jnp.sum(jnp.exp(scores - row_max), axis=-1, keepdims=True)))
            attn_probs = jnp.exp(scores - log_total)
            probs_bf = lax.optimization_barrier(attn_probs.astype(jnp.bfloat16)).astype(jnp.float32)
            head_out = jnp.einsum('sqk,ske->sqe', probs_bf, value_part)
            row_delta = lax.optimization_barrier(jnp.sum(grad_part * head_out, axis=-1, keepdims=True))
            prob_grads = jnp.einsum('sqe,ske->sqk', grad_part, value_part)
            score_grads = lax.optimization_barrier((score_scale * attn_probs * (prob_grads - row_delta)).astype(jnp.bfloat16)).astype(jnp.float32)
            query_grad = jnp.einsum('sqk,ske->sqe', score_grads, key_part).astype(jnp.bfloat16)
            key_grad = jnp.einsum('sqk,sqe->ske', score_grads, query_part).astype(jnp.bfloat16)
            value_grad = jnp.einsum('sqk,sqe->ske', probs_bf, grad_part).astype(jnp.bfloat16)
            head_outs.append(spread(head_out))
            query_grads.append(spread(query_grad))
            key_grads.append(spread(key_grad))
            value_grads.append(spread(value_grad))
    attention = jnp.stack(head_outs, axis=1).reshape(length, HEADS * HEAD_DIM).astype(jnp.bfloat16)
    result = jnp.dot(attention, w_out, preferred_element_type=jnp.float32).astype(jnp.bfloat16)
    query_rows = jnp.stack(query_grads, axis=1).reshape(length, HEADS * HEAD_DIM)
    key_rows = jnp.stack(key_grads, axis=1).reshape(length, HEADS * HEAD_DIM)
    value_rows = jnp.stack(value_grads, axis=1).reshape(length, HEADS * HEAD_DIM)
    token_grads = (jnp.dot(query_rows, w_query.T, preferred_element_type=jnp.float32) + jnp.dot(key_rows, w_key.T, preferred_element_type=jnp.float32) + jnp.dot(value_rows, w_value.T, preferred_element_type=jnp.float32)).astype(jnp.bfloat16)
    local_sums = jnp.stack([jnp.dot(tokens.T, query_rows, preferred_element_type=jnp.float32), jnp.dot(tokens.T, key_rows, preferred_element_type=jnp.float32), jnp.dot(tokens.T, value_rows, preferred_element_type=jnp.float32), jnp.dot(attention.T, result_grad, preferred_element_type=jnp.float32)])
    return (result, token_grads, local_sums)

def reference(tokens, valid_mask, w_query, w_key, w_value, w_out, result_grad):

    def apply_one(inputs):
        return one_sequence(inputs, w_query, w_key, w_value, w_out)
    result, token_grads, local_sums = lax.map(apply_one, (tokens, valid_mask, result_grad))
    return (result, token_grads, lax.optimization_barrier(jnp.sum(local_sums, axis=0)))
```

```python
import functools
import math

import jax
import jax.numpy as jnp
from jax import lax
from jax.experimental import pallas as pl
from jax.experimental.pallas import tpu as pltpu
from jax.sharding import PartitionSpec as P

HEADS = 16
HEAD_DIM = 48
GROUPS = 4
PER_GROUP = HEADS // GROUPS
LANES = 128
HALF = 64
WINDOW = 256
MASKED = -1e30
F32 = jnp.float32
BF16 = jnp.bfloat16
MESH = pl.DeviceIdType.MESH


def dot_nn(a, b):
    return lax.dot_general(a, b, (((1,), (0,)), ((), ())), preferred_element_type=F32)


def dot_nt(a, b):
    return lax.dot_general(a, b, (((1,), (1,)), ((), ())), preferred_element_type=F32)


def dot_tn(a, b):
    return lax.dot_general(a, b, (((0,), (0,)), ((), ())), preferred_element_type=F32)


class Plan:
    def __init__(self, seq, length):
        self.seq = seq
        self.length = length
        self.sizes = [seq * 2**g // 2 ** (GROUPS - 1) for g in range(GROUPS)]
        self.rows = [length // 2**g for g in range(GROUPS)]
        self.unit_rows = self.sizes[0] * length
        self.first_slot = []
        slots = 0
        for size in self.sizes:
            if size <= PER_GROUP:
                self.first_slot.append(slots)
                slots += PER_GROUP // size
            else:
                self.first_slot.append(None)
        self.extra = slots
        self.slots = slots + 1

    def start(self, group, head):
        quarter = self.length // 4
        if group == 0:
            return 0
        if group == 1:
            return head % 2 * (2 * quarter)
        return head % 2 * (2 * quarter) + head // 2 * quarter

    def place(self, group, head, base):
        size = self.sizes[group]
        if size <= PER_GROUP:
            each = PER_GROUP // size
            return base + head // each, self.first_slot[group] + head % each
        stride = size // PER_GROUP
        return base + head * stride + stride // 2 - 1, self.extra

    def groups_of_slot(self, slot):
        if slot == self.extra:
            return [(g, 0) for g in range(GROUPS) if self.sizes[g] > PER_GROUP]
        for g in reversed(range(GROUPS)):
            if self.first_slot[g] is not None and slot >= self.first_slot[g]:
                return [(g, slot - self.first_slot[g])]

    def owned(self, group, index, me):
        size = self.sizes[group]
        if size <= PER_GROUP:
            each = PER_GROUP // size
            return None, me % size * each + index
        stride = size // PER_GROUP
        return me % stride == stride // 2 - 1, me % size // stride


def guarded(condition, body):
    if condition is None:
        body()
    else:
        pl.when(condition)(body)


def spread_matrix(offset, high):
    row = lax.broadcasted_iota(jnp.int32, (WINDOW, PER_GROUP * LANES), 0)
    col = lax.broadcasted_iota(jnp.int32, (WINDOW, PER_GROUP * LANES), 1)
    lane = (col & (LANES - 1)) - (HALF if high else 0)
    head = col >> 7
    hit = (lane >= 0) & (lane < HEAD_DIM) & (row == offset + HEAD_DIM * head + lane)
    return hit.astype(F32).astype(BF16)


def window_of(group):
    first = group * PER_GROUP * HEAD_DIM
    begin = first // LANES * LANES
    return begin, first - begin


def permutation(length):
    eighth = length // 8
    bits = eighth.bit_length() - 1
    row = lax.broadcasted_iota(jnp.int32, (length, length), 0)
    col = lax.broadcasted_iota(jnp.int32, (length, length), 1)
    block = row >> bits
    residue = ((block & 1) << 2) | (block & 2) | (block >> 2)
    return col == ((row & (eighth - 1)) << 3) + residue


def attend(units, outs, slot, scale):
    tile0 = units[slot, 0]
    tile1 = units[slot, 1]
    low = lax.broadcasted_iota(jnp.int32, tile0.shape, 1) < HALF
    zero = jnp.zeros_like(tile0)
    scores = dot_nt(jnp.where(low, tile0, zero), tile1) * scale
    top = jnp.max(scores, axis=-1, keepdims=True)
    weights = jnp.exp(scores - top)
    probs = weights * (1.0 / jnp.sum(weights, axis=-1, keepdims=True))
    probs_bf = probs.astype(BF16)
    head_out = dot_nn(probs_bf, tile1)
    grad = jnp.where(low, zero, tile0)
    delta = jnp.sum(grad.astype(F32) * head_out, axis=-1, keepdims=True)
    score_grads = (scale * probs * (dot_nt(grad, tile1) - delta)).astype(BF16)
    outs[slot, 0] = jnp.where(low, dot_nn(score_grads, tile1), head_out).astype(BF16)
    outs[slot, 1] = jnp.where(low, dot_tn(score_grads, tile0), dot_tn(probs_bf, tile0)).astype(BF16)


def layer_kernel(plan, rows_each, *refs):
    (x_ref, mask_ref, wq_ref, wk_ref, wv_ref, wo_ref, g_ref) = refs[:7]
    result_ref, tgrad_ref, wgrad_ref = refs[7:10]
    staged = refs[10 : 10 + GROUPS]
    (units, outs, back, acc, send_sem, recv_sem, ret_send, ret_recv) = refs[10 + GROUPS :]
    length, seq = plan.length, plan.seq
    scale = 1.0 / math.sqrt(HEAD_DIM)
    me = lax.axis_index("seq")

    back[...] = jnp.zeros_like(back)
    barrier = pltpu.get_barrier_semaphore()
    for step in range(1, seq):
        pl.semaphore_signal(
            barrier, inc=1, device_id={"seq": lax.rem(me + step, seq)}, device_id_type=MESH
        )

    perm = permutation(length)
    perm_f = perm.astype(F32)
    perm_bf = perm_f.astype(BF16)
    x = dot_nn(perm_bf, x_ref[...]).astype(BF16)
    g = dot_nn(perm_bf, g_ref[...]).astype(BF16)
    bias_row = jnp.where(mask_ref[...] == 1, 0.0, MASKED)
    bias = jnp.sum(jnp.where(perm, jnp.broadcast_to(bias_row, perm.shape), 0.0), axis=1, keepdims=True)
    queries = dot_nn(x, wq_ref[...]).astype(BF16)
    keys = dot_nn(x, wk_ref[...]).astype(BF16)
    values = dot_nn(x, wv_ref[...]).astype(BF16)
    grads = dot_nt(g, wo_ref[...]).astype(BF16)
    lane = lax.broadcasted_iota(jnp.int32, (length, PER_GROUP * LANES), 1) & (LANES - 1)
    spreads = {}
    for group in range(GROUPS):
        begin, offset = window_of(group)
        if offset not in spreads:
            spreads[offset] = (spread_matrix(offset, False), spread_matrix(offset, True))
    for group in reversed(range(GROUPS)):
        begin, offset = window_of(group)
        low, high = spreads[offset]
        cut = slice(begin, begin + WINDOW)
        tile0 = dot_nn(queries[:, cut], low) + dot_nn(grads[:, cut], high)
        tile1 = dot_nn(keys[:, cut], low) + dot_nn(values[:, cut], high)
        tile0 = jnp.where(lane == HEAD_DIM, 1.0, tile0).astype(BF16)
        tile1 = jnp.where(lane == HEAD_DIM, bias, tile1).astype(BF16)
        for head in range(PER_GROUP):
            first = plan.start(group, head)
            rows = slice(first, first + plan.rows[group])
            lanes = slice(head * LANES, (head + 1) * LANES)
            staged[group][head, 0] = tile0[rows, lanes]
            staged[group][head, 1] = tile1[rows, lanes]

    pl.semaphore_wait(barrier, seq - 1)

    def out_copies(group):
        size = plan.sizes[group]
        base = me - me % size
        rows = plan.rows[group]
        row = pl.multiple_of(me % size * rows, rows)
        for head in range(PER_GROUP):
            owner, slot = plan.place(group, head, base)
            source = staged[group].at[head]
            target = units.at[slot, :, pl.ds(row, rows), :]
            remote = functools.partial(
                pltpu.make_async_remote_copy,
                source, target, send_sem.at[group, head], recv_sem.at[slot],
                device_id={"seq": owner}, device_id_type=MESH,
            )
            local = functools.partial(pltpu.make_async_copy, source, target, recv_sem.at[slot])
            yield owner, remote, local

    for group in reversed(range(GROUPS)):
        for owner, remote, local in out_copies(group):
            pl.when(owner != me)(lambda: remote().start())
            pl.when(owner == me)(lambda: local().start())

    def returns(slot, group, index, head):
        size = plan.sizes[group]
        base = me - me % size
        rows = plan.rows[group]
        first = pl.multiple_of(plan.start(group, head), plan.length // 8)
        for step in range(size):
            j = lax.rem(me + step, size)
            source = outs.at[slot, :, pl.ds(pl.multiple_of(j * rows, rows), rows), :]
            target = back.at[group, head, :, pl.ds(first, rows), :]
            if step == 0:
                yield None, pltpu.make_async_copy(source, target, ret_recv.at[group])
            else:
                yield step, pltpu.make_async_remote_copy(
                    source, target, ret_send.at[slot, step], ret_recv.at[group],
                    device_id={"seq": base + j}, device_id_type=MESH,
                )

    def start_all(slot, group, index, head):
        for _, copy in returns(slot, group, index, head):
            copy.start()

    def wait_sends(slot, group, index, head):
        for step, copy in returns(slot, group, index, head):
            if step is not None:
                copy.wait_send()

    order = list(range(plan.slots))
    for slot in order:
        entries = plan.groups_of_slot(slot)
        if not entries:
            continue
        owned = [(group, index) + plan.owned(group, index, me) for group, index in entries]
        conditions = [o[2] for o in owned if o[2] is not None]
        active = functools.reduce(jnp.logical_or, conditions) if conditions else None

        def work(slot=slot):
            pltpu.make_async_copy(units.at[slot], units.at[slot], recv_sem.at[slot]).wait()
            attend(units, outs, slot, scale)

        guarded(active, work)
        for group, index, condition, head in owned:
            guarded(condition, functools.partial(start_all, slot, group, index, head))

    for group in reversed(range(GROUPS)):
        for owner, remote, local in out_copies(group):
            pl.when(owner != me)(lambda: remote().wait_send())

    acc[...] = jnp.zeros_like(acc)
    for group in range(GROUPS):
        pltpu.make_async_copy(staged[group], staged[group], ret_recv.at[group]).wait()
        begin, offset = window_of(group)
        low, high = spreads[offset]
        for tile in range(2):
            packed = jnp.concatenate([back[group, head, tile] for head in range(PER_GROUP)], axis=1)
            acc[2 * tile, :, begin : begin + WINDOW] += dot_nt(packed, low)
            acc[2 * tile + 1, :, begin : begin + WINDOW] += dot_nt(packed, high)
    for slot in order:
        for group, index in plan.groups_of_slot(slot):
            condition, head = plan.owned(group, index, me)
            guarded(condition, functools.partial(wait_sends, slot, group, index, head))

    query_rows = acc[0].astype(BF16)
    attention = acc[1].astype(BF16)
    key_rows = acc[2].astype(BF16)
    value_rows = acc[3].astype(BF16)
    pairs = [(x, query_rows), (x, key_rows), (x, value_rows), (attention, g)]
    for which, (left, right) in enumerate(pairs):
        product = dot_tn(left, right).astype(wgrad_ref.dtype)
        for target in range(seq):
            wgrad_ref[target, which] = product[target * rows_each : (target + 1) * rows_each]
    result = dot_nn(attention, wo_ref[...]).astype(BF16)
    result_ref[...] = dot_tn(perm_bf, result).astype(BF16)
    token = (
        dot_nt(query_rows, wq_ref[...])
        + dot_nt(key_rows, wk_ref[...])
        + dot_nt(value_rows, wv_ref[...])
    ).astype(BF16)
    tgrad_ref[...] = dot_tn(perm_bf, token).astype(BF16)


def run_layer(seq, x, mask, wq, wk, wv, wo, g, wgrad_dtype):
    length, width = x.shape
    plan = Plan(seq, length)
    rows_each = width // seq
    vmem = pl.BlockSpec(memory_space=pltpu.VMEM)
    return pl.pallas_call(
        functools.partial(layer_kernel, plan, rows_each),
        out_shape=(
            jax.ShapeDtypeStruct((length, width), BF16),
            jax.ShapeDtypeStruct((length, width), BF16),
            jax.ShapeDtypeStruct((seq, 4, rows_each, width), wgrad_dtype),
        ),
        in_specs=[vmem] * 7,
        out_specs=[vmem] * 3,
        scratch_shapes=[
            pltpu.VMEM((PER_GROUP, 2, plan.rows[group], LANES), BF16) for group in range(GROUPS)
        ]
        + [
            pltpu.VMEM((plan.slots, 2, plan.unit_rows, LANES), BF16),
            pltpu.VMEM((plan.slots, 2, plan.unit_rows, LANES), BF16),
            pltpu.VMEM((GROUPS, PER_GROUP, 2, length, LANES), BF16),
            pltpu.VMEM((4, length, width), F32),
            pltpu.SemaphoreType.DMA((GROUPS, PER_GROUP)),
            pltpu.SemaphoreType.DMA((plan.slots,)),
            pltpu.SemaphoreType.DMA((plan.slots, seq)),
            pltpu.SemaphoreType.DMA((GROUPS,)),
        ],
        compiler_params=pltpu.CompilerParams(
            collective_id=0, has_side_effects=True, vmem_limit_bytes=60 * 2**20
        ),
        name="layer",
    )(x, mask, wq, wk, wv, wo, g)


BITS = 4
STREAMS = ((1, 2, 3), (2, 3, 1))


def reduce_kernel(parts, out_ref, data, *refs):
    recvs = refs[:-3]
    send_sem, recv_sem, load_sem = refs[-3:]
    me = lax.axis_index("seq")
    dp = lax.axis_index("dp")
    bit = [me // 2**k % 2 for k in range(BITS)]
    barrier = pltpu.get_barrier_semaphore()
    for k in range(BITS):
        pl.semaphore_signal(
            barrier, inc=1, device_id={"seq": me + 2**k - bit[k] * 2 ** (k + 1)}, device_id_type=MESH
        )
    pl.semaphore_signal(barrier, inc=1, device_id={"dp": 1 - dp}, device_id_type=MESH)
    load = pltpu.make_async_copy(parts, data, load_sem)
    load.start()
    load.wait()
    pl.semaphore_wait(barrier, BITS + 1)

    def view(fixed, m):
        index = [fixed.get(3 - d, slice(None)) for d in range(BITS)]
        return tuple(index) + (m,)

    def send(number, k, done, stream):
        fixed = {b: bit[b] for b in done}
        fixed[k] = 1 - bit[k]
        return pltpu.make_async_remote_copy(
            data.at[view(fixed, pl.ds(2 * stream, 2))], recvs[number], send_sem.at[number],
            recv_sem.at[number],
            device_id={"seq": me + 2**k - bit[k] * 2 ** (k + 1)}, device_id_type=MESH,
        )

    def add(number, k, done, stream):
        fixed = {b: bit[b] for b in done}
        fixed[k] = bit[k]
        mine = view(fixed, pl.ds(2 * stream, 2))
        data[mine] = (data[mine].astype(F32) + recvs[number][...].astype(F32)).astype(BF16)

    sequences = [(0,) + s for s in STREAMS]
    copies = []
    for stage in range(BITS):
        for stream in range(2):
            number = stage * 2 + stream
            if stage > 0:
                before = number - 2
                copies[before].wait_recv()
                add(before, sequences[stream][stage - 1], sequences[stream][: stage - 1], stream)
            copies.append(send(number, sequences[stream][stage], sequences[stream][:stage], stream))
            copies[-1].start()
    final = []
    for stream in range(2):
        before = (BITS - 1) * 2 + stream
        number = BITS * 2 + stream
        copies[before].wait_recv()
        add(before, sequences[stream][BITS - 1], sequences[stream][: BITS - 1], stream)
        mine = view(dict(enumerate(bit)), pl.ds(2 * stream, 2))
        final.append(
            pltpu.make_async_remote_copy(
                data.at[mine], recvs[number], send_sem.at[number], recv_sem.at[number],
                device_id={"dp": 1 - dp}, device_id_type=MESH,
            )
        )
        final[-1].start()
    for stream in range(2):
        mine = view(dict(enumerate(bit)), pl.ds(2 * stream, 2))
        final[stream].wait_recv()
        out_ref[2 * stream : 2 * stream + 2] = (
            data[mine].astype(F32) + recvs[BITS * 2 + stream][...].astype(F32)
        )
    for copy in copies + final:
        copy.wait_send()


def reduce_parts(parts, rows_each, width):
    parts = parts.reshape(2, 2, 2, 2, 4, rows_each, width)
    recvs = []
    for stage in range(BITS):
        recvs += [pltpu.VMEM((2,) * (BITS - 1 - stage) + (2, rows_each, width), BF16)] * 2
    recvs += [pltpu.VMEM((2, rows_each, width), BF16)] * 2
    return pl.pallas_call(
        reduce_kernel,
        out_shape=jax.ShapeDtypeStruct((4, rows_each, width), F32),
        in_specs=[pl.BlockSpec(memory_space=pl.ANY)],
        out_specs=pl.BlockSpec(memory_space=pltpu.VMEM),
        scratch_shapes=[pltpu.VMEM(parts.shape, BF16)]
        + recvs
        + [
            pltpu.SemaphoreType.DMA((2 * BITS + 2,)),
            pltpu.SemaphoreType.DMA((2 * BITS + 2,)),
            pltpu.SemaphoreType.DMA,
        ],
        compiler_params=pltpu.CompilerParams(
            collective_id=1, has_side_effects=True, vmem_limit_bytes=60 * 2**20
        ),
        name="reduce",
    )(parts)


def per_device(tokens, valid_mask, w_query, w_key, w_value, w_out, result_grad):
    seq, dp = lax.axis_size("seq"), lax.axis_size("dp")
    width = tokens.shape[2]
    rows_each = width // seq
    direct = seq == 2**BITS and dp == 2
    result, token_grads, parts = run_layer(
        seq, tokens[0], valid_mask, w_query, w_key, w_value, w_out, result_grad[0],
        BF16 if direct else F32,
    )
    if direct:
        weight_grads = reduce_parts(parts, rows_each, width)
    else:
        content = parts.reshape(seq, dp, -1).transpose(1, 0, 2).reshape(-1)
        share = lax.psum_scatter(content, ("dp", "seq"), scatter_dimension=0, tiled=True)
        weight_grads = lax.all_gather(share, "dp", axis=0, tiled=True).reshape(4, rows_each, width)
    return (result[None], token_grads[None], weight_grads)


def solution(mesh):
    return jax.shard_map(
        per_device,
        mesh=mesh,
        in_specs=(P("dp", "seq", None), P("dp", "seq"), P(), P(), P(), P(), P("dp", "seq", None)),
        out_specs=(P("dp", "seq", None), P("dp", "seq", None), P(None, "seq", None)),
        check_vma=False,
    )
```

```python
import functools
import math

import jax
import jax.numpy as jnp
from jax import lax
from jax.experimental import pallas as pl
from jax.experimental.pallas import tpu as pltpu
from jax.sharding import PartitionSpec as P

HEADS = 16
HEAD_DIM = 48
GROUPS = 4
PER_GROUP = HEADS // GROUPS
LANES = 128
HALF = 64
WINDOW = 256
MASKED = -1e30
F32 = jnp.float32
BF16 = jnp.bfloat16
MESH = pl.DeviceIdType.MESH


def dot_nn(a, b):
    return lax.dot_general(a, b, (((1,), (0,)), ((), ())), preferred_element_type=F32)


def dot_nt(a, b):
    return lax.dot_general(a, b, (((1,), (1,)), ((), ())), preferred_element_type=F32)


def dot_tn(a, b):
    return lax.dot_general(a, b, (((0,), (0,)), ((), ())), preferred_element_type=F32)


class Plan:
    def __init__(self, seq, length):
        self.seq = seq
        self.length = length
        self.sizes = [seq * 2**g // 2 ** (GROUPS - 1) for g in range(GROUPS)]
        self.rows = [length // 2**g for g in range(GROUPS)]
        self.unit_rows = self.sizes[0] * length
        self.first_slot = []
        slots = 0
        for size in self.sizes:
            if size <= PER_GROUP:
                self.first_slot.append(slots)
                slots += PER_GROUP // size
            else:
                self.first_slot.append(None)
        self.extra = slots
        self.slots = slots + 1

    def start(self, group, head):
        quarter = self.length // 4
        if group == 0:
            return 0
        if group == 1:
            return head % 2 * (2 * quarter)
        return head % 2 * (2 * quarter) + head // 2 * quarter

    def place(self, group, head, base):
        size = self.sizes[group]
        if size <= PER_GROUP:
            each = PER_GROUP // size
            return base + head // each, self.first_slot[group] + head % each
        stride = size // PER_GROUP
        return base + head * stride + stride // 2 - 1, self.extra

    def groups_of_slot(self, slot):
        if slot == self.extra:
            return [(g, 0) for g in range(GROUPS) if self.sizes[g] > PER_GROUP]
        for g in reversed(range(GROUPS)):
            if self.first_slot[g] is not None and slot >= self.first_slot[g]:
                return [(g, slot - self.first_slot[g])]

    def owned(self, group, index, me):
        size = self.sizes[group]
        if size <= PER_GROUP:
            each = PER_GROUP // size
            return None, me % size * each + index
        stride = size // PER_GROUP
        return me % stride == stride // 2 - 1, me % size // stride


def guarded(condition, body):
    if condition is None:
        body()
    else:
        pl.when(condition)(body)


def spread_matrix(offset, high):
    row = lax.broadcasted_iota(jnp.int32, (WINDOW, PER_GROUP * LANES), 0)
    col = lax.broadcasted_iota(jnp.int32, (WINDOW, PER_GROUP * LANES), 1)
    lane = (col & (LANES - 1)) - (HALF if high else 0)
    head = col >> 7
    hit = (lane >= 0) & (lane < HEAD_DIM) & (row == offset + HEAD_DIM * head + lane)
    return hit.astype(F32).astype(BF16)


def window_of(group):
    first = group * PER_GROUP * HEAD_DIM
    begin = first // LANES * LANES
    return begin, first - begin


def permutation(length):
    eighth = length // 8
    bits = eighth.bit_length() - 1
    row = lax.broadcasted_iota(jnp.int32, (length, length), 0)
    col = lax.broadcasted_iota(jnp.int32, (length, length), 1)
    block = row >> bits
    residue = ((block & 1) << 2) | (block & 2) | (block >> 2)
    return col == ((row & (eighth - 1)) << 3) + residue


def attend(units, outs, slot, scale):
    tile0 = units[slot, 0]
    tile1 = units[slot, 1]
    low = lax.broadcasted_iota(jnp.int32, tile0.shape, 1) < HALF
    zero = jnp.zeros_like(tile0)
    scores = dot_nt(jnp.where(low, tile0, zero), tile1) * scale
    top = jnp.max(scores, axis=-1, keepdims=True)
    weights = jnp.exp(scores - top)
    probs = weights * (1.0 / jnp.sum(weights, axis=-1, keepdims=True))
    probs_bf = probs.astype(BF16)
    head_out = dot_nn(probs_bf, tile1)
    grad = jnp.where(low, zero, tile0)
    delta = jnp.sum(grad.astype(F32) * head_out, axis=-1, keepdims=True)
    score_grads = (scale * probs * (dot_nt(grad, tile1) - delta)).astype(BF16)
    outs[slot, 0] = jnp.where(low, dot_nn(score_grads, tile1), head_out).astype(BF16)
    outs[slot, 1] = jnp.where(low, dot_tn(score_grads, tile0), dot_tn(probs_bf, tile0)).astype(BF16)


BITS = 4
CHUNK = 16
Y = BITS
FIRST_X, FIRST_Y, FIRST_Z = (1, Y, 2, 3), (Y, 1, 2, 3), (2, 3, 1, Y)


def chunk_orders(rows_each):
    pattern = (FIRST_Z, FIRST_X, FIRST_Y)
    chunks = []
    for which in range(4):
        for index in range(rows_each // CHUNK):
            order = pattern[index % 3]
            if which == 3 and order is FIRST_Z:
                order = FIRST_X
            chunks.append((which, index * CHUNK, order))
    return chunks


def chunk_shapes(rows_each, width):
    shapes = []
    for _, _, order in chunk_orders(rows_each):
        open_dims = {3, 2, 1, Y}
        for axis in order:
            open_dims.remove(axis)
            shapes.append((2,) * len(open_dims) + (CHUNK, width // 2))
    return shapes


class Reducer:
    def __init__(self, rows_each, data, core, final, recvs, core_sems, sems, final_sems):
        self.data, self.core, self.final, self.recvs = data, core, final, recvs
        self.core_sems, self.sems, self.final_sems = core_sems, sems, final_sems
        self.chunks = chunk_orders(rows_each)
        self.me = lax.axis_index("seq")
        self.dp = lax.axis_index("dp")
        self.bit = [self.me // 2**k % 2 for k in range(BITS)] + [self.dp]
        self.started = []
        self.current = {}

    def peer(self, axis):
        if axis == Y:
            return {"dp": 1 - self.dp}
        return {"seq": self.me + 2**axis - self.bit[axis] * 2 ** (axis + 1)}

    def view(self, fixed, which, rows):
        index = [fixed.get(3 - d, slice(None)) for d in range(BITS)]
        return tuple(index) + (which, fixed.get(Y, slice(None)), rows)

    def copy(self, source, target, sems, number, axis):
        copy = pltpu.make_async_remote_copy(
            source, target, sems.at[0, number], sems.at[1, number],
            device_id=self.peer(axis), device_id_type=MESH,
        )
        copy.start()
        self.started.append(copy)
        return copy

    def core_start(self, which):
        other = self.view({0: 1 - self.bit[0]}, which, slice(None))
        self.current["core", which] = self.copy(
            self.data.at[other], self.core.at[which], self.core_sems, which, 0
        )

    def core_add(self, which):
        self.current["core", which].wait_recv()
        mine = self.view({0: self.bit[0]}, which, slice(None))
        self.data[mine] = (
            self.data[mine].astype(F32) + self.core[which].astype(F32)
        ).astype(BF16)

    def fixed(self, order, stage):
        return {axis: self.bit[axis] for axis in (0,) + order[:stage]}

    def start(self, number, stage):
        which, row, order = self.chunks[number]
        rows = pl.ds(row, CHUNK)
        if stage == len(order):
            mine = self.view(self.fixed(order, stage), which, rows)
            self.current[number] = self.copy(
                self.data.at[mine], self.final.at[which, rows], self.final_sems, number, Y
            )
            return
        fixed = self.fixed(order, stage)
        fixed[order[stage]] = 1 - self.bit[order[stage]]
        slot = number * len(order) + stage
        self.current[number] = self.copy(
            self.data.at[self.view(fixed, which, rows)], self.recvs[slot], self.sems, slot,
            order[stage],
        )

    def add(self, number, stage):
        self.current[number].wait_recv()
        which, row, order = self.chunks[number]
        mine = self.view(self.fixed(order, stage + 1), which, pl.ds(row, CHUNK))
        got = self.recvs[number * len(order) + stage][...]
        self.data[mine] = (self.data[mine].astype(F32) + got.astype(F32)).astype(BF16)

    def numbers(self, which):
        return [n for n, chunk in enumerate(self.chunks) if chunk[0] == which]

    def finish(self, out_ref):
        numbers = sorted(range(len(self.chunks)), key=lambda n: self.chunks[n][2] is FIRST_Z)
        for stage in range(4):
            for number in numbers:
                self.add(number, stage)
                self.start(number, stage + 1)
        for number in numbers:
            self.current[number].wait_recv()
        own_at = self.view(dict(enumerate(self.bit)), slice(None), slice(None))
        own = self.data[own_at].astype(F32)
        other = self.final[...].astype(F32)
        half = out_ref.shape[2] // 2
        low = self.dp == 0
        out_ref[:, :, :half] = jnp.where(low, own, other)
        out_ref[:, :, half:] = jnp.where(low, other, own)
        for copy in self.started:
            copy.wait_send()


def layer_kernel(plan, rows_each, direct, *refs):
    (x_ref, mask_ref, *weight_hbm, g_ref) = refs[:7]
    result_ref, tgrad_ref, wgrad_ref = refs[7:10]
    staged = refs[10 : 10 + GROUPS]
    refs = refs[10 + GROUPS :]
    (units, outs, back, acc, send_sem, recv_sem, ret_send, ret_recv, weights, load_sem) = refs[:10]
    length, seq = plan.length, plan.seq
    scale = 1.0 / math.sqrt(HEAD_DIM)
    me = lax.axis_index("seq")

    loads = [
        pltpu.make_async_copy(weight_hbm[k], weights.at[k], load_sem.at[k]) for k in range(4)
    ]
    for load in loads:
        load.start()
    back[...] = jnp.zeros_like(back)
    barrier = pltpu.get_barrier_semaphore()
    for step in range(1, seq):
        pl.semaphore_signal(
            barrier, inc=1, device_id={"seq": lax.rem(me + step, seq)}, device_id_type=MESH
        )
    if direct:
        pl.semaphore_signal(
            barrier, inc=1, device_id={"dp": 1 - lax.axis_index("dp")}, device_id_type=MESH
        )

    perm = permutation(length)
    perm_f = perm.astype(F32)
    perm_bf = perm_f.astype(BF16)
    x = dot_nn(perm_bf, x_ref[...]).astype(BF16)
    g = dot_nn(perm_bf, g_ref[...]).astype(BF16)
    bias_row = jnp.where(mask_ref[...] == 1, 0.0, MASKED)
    bias = jnp.sum(jnp.where(perm, jnp.broadcast_to(bias_row, perm.shape), 0.0), axis=1, keepdims=True)
    loads[0].wait()
    queries = dot_nn(x, weights[0]).astype(BF16)
    loads[1].wait()
    keys = dot_nn(x, weights[1]).astype(BF16)
    loads[2].wait()
    values = dot_nn(x, weights[2]).astype(BF16)
    loads[3].wait()
    grads = dot_nt(g, weights[3]).astype(BF16)
    lane = lax.broadcasted_iota(jnp.int32, (length, PER_GROUP * LANES), 1) & (LANES - 1)
    spreads = {}
    for group in range(GROUPS):
        begin, offset = window_of(group)
        if offset not in spreads:
            spreads[offset] = (spread_matrix(offset, False), spread_matrix(offset, True))
    for group in reversed(range(GROUPS)):
        begin, offset = window_of(group)
        low, high = spreads[offset]
        cut = slice(begin, begin + WINDOW)
        tile0 = dot_nn(queries[:, cut], low) + dot_nn(grads[:, cut], high)
        tile1 = dot_nn(keys[:, cut], low) + dot_nn(values[:, cut], high)
        tile0 = jnp.where(lane == HEAD_DIM, 1.0, tile0).astype(BF16)
        tile1 = jnp.where(lane == HEAD_DIM, bias, tile1).astype(BF16)
        for head in range(PER_GROUP):
            first = plan.start(group, head)
            rows = slice(first, first + plan.rows[group])
            lanes = slice(head * LANES, (head + 1) * LANES)
            staged[group][head, 0] = tile0[rows, lanes]
            staged[group][head, 1] = tile1[rows, lanes]

    pl.semaphore_wait(barrier, seq - 1 + (1 if direct else 0))

    def out_copies(group):
        size = plan.sizes[group]
        base = me - me % size
        rows = plan.rows[group]
        row = pl.multiple_of(me % size * rows, rows)
        for head in range(PER_GROUP):
            owner, slot = plan.place(group, head, base)
            source = staged[group].at[head]
            target = units.at[slot, :, pl.ds(row, rows), :]
            remote = functools.partial(
                pltpu.make_async_remote_copy,
                source, target, send_sem.at[group, head], recv_sem.at[slot],
                device_id={"seq": owner}, device_id_type=MESH,
            )
            local = functools.partial(pltpu.make_async_copy, source, target, recv_sem.at[slot])
            yield owner, remote, local

    for group in reversed(range(GROUPS)):
        for owner, remote, local in out_copies(group):
            pl.when(owner != me)(lambda: remote().start())
            pl.when(owner == me)(lambda: local().start())

    def returns(slot, group, index, head):
        size = plan.sizes[group]
        base = me - me % size
        rows = plan.rows[group]
        first = pl.multiple_of(plan.start(group, head), plan.length // 8)
        for step in range(size):
            j = lax.rem(me + step, size)
            source = outs.at[slot, :, pl.ds(pl.multiple_of(j * rows, rows), rows), :]
            target = back.at[group, head, :, pl.ds(first, rows), :]
            if step == 0:
                yield None, pltpu.make_async_copy(source, target, ret_recv.at[group])
            else:
                yield step, pltpu.make_async_remote_copy(
                    source, target, ret_send.at[slot, step], ret_recv.at[group],
                    device_id={"seq": base + j}, device_id_type=MESH,
                )

    def start_all(slot, group, index, head):
        for _, copy in returns(slot, group, index, head):
            copy.start()

    def wait_sends(slot, group, index, head):
        for step, copy in returns(slot, group, index, head):
            if step is not None:
                copy.wait_send()

    order = list(range(plan.slots))
    for slot in order:
        entries = plan.groups_of_slot(slot)
        if not entries:
            continue
        owned = [(group, index) + plan.owned(group, index, me) for group, index in entries]
        conditions = [o[2] for o in owned if o[2] is not None]
        active = functools.reduce(jnp.logical_or, conditions) if conditions else None

        def work(slot=slot):
            pltpu.make_async_copy(units.at[slot], units.at[slot], recv_sem.at[slot]).wait()
            attend(units, outs, slot, scale)

        guarded(active, work)
        for group, index, condition, head in owned:
            guarded(condition, functools.partial(start_all, slot, group, index, head))

    for group in reversed(range(GROUPS)):
        for owner, remote, local in out_copies(group):
            pl.when(owner != me)(lambda: remote().wait_send())

    acc[...] = jnp.zeros_like(acc)
    for group in range(GROUPS):
        pltpu.make_async_copy(staged[group], staged[group], ret_recv.at[group]).wait()
        begin, offset = window_of(group)
        low, high = spreads[offset]
        for tile in range(2):
            packed = jnp.concatenate([back[group, head, tile] for head in range(PER_GROUP)], axis=1)
            acc[2 * tile, :, begin : begin + WINDOW] += dot_nt(packed, low)
            acc[2 * tile + 1, :, begin : begin + WINDOW] += dot_nt(packed, high)
    for slot in order:
        for group, index in plan.groups_of_slot(slot):
            condition, head = plan.owned(group, index, me)
            guarded(condition, functools.partial(wait_sends, slot, group, index, head))

    query_rows = acc[0].astype(BF16)
    attention = acc[1].astype(BF16)
    key_rows = acc[2].astype(BF16)
    value_rows = acc[3].astype(BF16)
    pairs = [(x, query_rows), (x, key_rows), (x, value_rows), (attention, g)]

    def products():
        result = dot_nn(attention, weights[3]).astype(BF16)
        result_ref[...] = dot_tn(perm_bf, result).astype(BF16)
        token = (
            dot_nt(query_rows, weights[0])
            + dot_nt(key_rows, weights[1])
            + dot_nt(value_rows, weights[2])
        ).astype(BF16)
        tgrad_ref[...] = dot_tn(perm_bf, token).astype(BF16)

    if not direct:
        for which, (left, right) in enumerate(pairs):
            product = dot_tn(left, right)
            for target in range(seq):
                wgrad_ref[target, which] = product[target * rows_each : (target + 1) * rows_each]
        products()
        return

    data, core, final, core_sems, sems, final_sems, *recvs = refs[10:]
    reducer = Reducer(rows_each, data, core, final, recvs, core_sems, sems, final_sems)
    half = x_ref.shape[1] // 2

    def second(which):
        reducer.core_add(which)
        for number in reducer.numbers(which):
            reducer.start(number, 0)

    for which, (left, right) in enumerate(pairs):
        product = dot_tn(left, right).astype(BF16)
        for target in range(seq):
            bits = tuple(target >> k & 1 for k in (3, 2, 1, 0))
            rows = product[target * rows_each : (target + 1) * rows_each]
            data[bits + (which, 0)] = rows[:, :half]
            data[bits + (which, 1)] = rows[:, half:]
        reducer.core_start(which)
        if which > 0:
            second(which - 1)
    products()
    second(3)
    reducer.finish(wgrad_ref)


def run_layer(seq, x, mask, wq, wk, wv, wo, g, direct):
    length, width = x.shape
    plan = Plan(seq, length)
    rows_each = width // seq
    vmem = pl.BlockSpec(memory_space=pltpu.VMEM)
    hbm = pl.BlockSpec(memory_space=pl.ANY)
    if direct:
        grads_shape = (4, rows_each, width)
        shapes = chunk_shapes(rows_each, width)
        chunks = len(chunk_orders(rows_each))
        extra = [
            pltpu.VMEM((2,) * BITS + (4, 2, rows_each, width // 2), BF16),
            pltpu.VMEM((4, 2, 2, 2, 2, rows_each, width // 2), BF16),
            pltpu.VMEM((4, rows_each, width // 2), BF16),
            pltpu.SemaphoreType.DMA((2, 4)),
            pltpu.SemaphoreType.DMA((2, len(shapes))),
            pltpu.SemaphoreType.DMA((2, chunks)),
        ] + [pltpu.VMEM(shape, BF16) for shape in shapes]
    else:
        grads_shape = (seq, 4, rows_each, width)
        extra = []
    return pl.pallas_call(
        functools.partial(layer_kernel, plan, rows_each, direct),
        out_shape=(
            jax.ShapeDtypeStruct((length, width), BF16),
            jax.ShapeDtypeStruct((length, width), BF16),
            jax.ShapeDtypeStruct(grads_shape, F32),
        ),
        in_specs=[vmem] * 2 + [hbm] * 4 + [vmem],
        out_specs=[vmem] * 3,
        scratch_shapes=[
            pltpu.VMEM((PER_GROUP, 2, plan.rows[group], LANES), BF16) for group in range(GROUPS)
        ]
        + [
            pltpu.VMEM((plan.slots, 2, plan.unit_rows, LANES), BF16),
            pltpu.VMEM((plan.slots, 2, plan.unit_rows, LANES), BF16),
            pltpu.VMEM((GROUPS, PER_GROUP, 2, length, LANES), BF16),
            pltpu.VMEM((4, length, width), F32),
            pltpu.SemaphoreType.DMA((GROUPS, PER_GROUP)),
            pltpu.SemaphoreType.DMA((plan.slots,)),
            pltpu.SemaphoreType.DMA((plan.slots, seq)),
            pltpu.SemaphoreType.DMA((GROUPS,)),
            pltpu.VMEM((4, width, width), BF16),
            pltpu.SemaphoreType.DMA((4,)),
        ]
        + extra,
        compiler_params=pltpu.CompilerParams(
            collective_id=0, has_side_effects=True, vmem_limit_bytes=60 * 2**20
        ),
        name="layer",
    )(x, mask, wq, wk, wv, wo, g)


def per_device(tokens, valid_mask, w_query, w_key, w_value, w_out, result_grad):
    seq, dp = lax.axis_size("seq"), lax.axis_size("dp")
    width = tokens.shape[2]
    rows_each = width // seq
    direct = seq == 2**BITS and dp == 2 and rows_each % CHUNK == 0
    result, token_grads, parts = run_layer(
        seq, tokens[0], valid_mask, w_query, w_key, w_value, w_out, result_grad[0],
        direct,
    )
    if direct:
        weight_grads = parts
    else:
        content = parts.reshape(seq, dp, -1).transpose(1, 0, 2).reshape(-1)
        share = lax.psum_scatter(content, ("dp", "seq"), scatter_dimension=0, tiled=True)
        weight_grads = lax.all_gather(share, "dp", axis=0, tiled=True).reshape(4, rows_each, width)
    return (result[None], token_grads[None], weight_grads)


def solution(mesh):
    return jax.shard_map(
        per_device,
        mesh=mesh,
        in_specs=(P("dp", "seq", None), P("dp", "seq"), P(), P(), P(), P(), P("dp", "seq", None)),
        out_specs=(P("dp", "seq", None), P("dp", "seq", None), P(None, "seq", None)),
        check_vma=False,
    )
```

```python
import functools
import math

import jax
import jax.numpy as jnp
from jax import lax
from jax.experimental import pallas as pl
from jax.experimental.pallas import tpu as pltpu
from jax.sharding import PartitionSpec as P

HEADS = 16
HEAD_DIM = 48
GROUPS = 4
PER_GROUP = HEADS // GROUPS
LANES = 128
HALF = 64
WINDOW = 256
MASKED = -1e30
F32 = jnp.float32
BF16 = jnp.bfloat16
MESH = pl.DeviceIdType.MESH


def dot_nn(a, b):
    return lax.dot_general(a, b, (((1,), (0,)), ((), ())), preferred_element_type=F32)


def dot_nt(a, b):
    return lax.dot_general(a, b, (((1,), (1,)), ((), ())), preferred_element_type=F32)


def dot_tn(a, b):
    return lax.dot_general(a, b, (((0,), (0,)), ((), ())), preferred_element_type=F32)


class Plan:
    def __init__(self, seq, length):
        self.seq = seq
        self.length = length
        self.sizes = [seq * 2**g // 2 ** (GROUPS - 1) for g in range(GROUPS)]
        self.rows = [length // 2**g for g in range(GROUPS)]
        self.unit_rows = self.sizes[0] * length
        self.first_slot = []
        slots = 0
        for size in self.sizes:
            if size <= PER_GROUP:
                self.first_slot.append(slots)
                slots += PER_GROUP // size
            else:
                self.first_slot.append(None)
        self.extra = slots
        self.slots = slots + 1

    def start(self, group, head):
        quarter = self.length // 4
        if group == 0:
            return 0
        if group == 1:
            return head % 2 * (2 * quarter)
        return head % 2 * (2 * quarter) + head // 2 * quarter

    def place(self, group, head, base):
        size = self.sizes[group]
        if size <= PER_GROUP:
            each = PER_GROUP // size
            return base + head // each, self.first_slot[group] + head % each
        stride = size // PER_GROUP
        return base + head * stride + stride // 2 - 1, self.extra

    def groups_of_slot(self, slot):
        if slot == self.extra:
            return [(g, 0) for g in range(GROUPS) if self.sizes[g] > PER_GROUP]
        for g in reversed(range(GROUPS)):
            if self.first_slot[g] is not None and slot >= self.first_slot[g]:
                return [(g, slot - self.first_slot[g])]

    def owned(self, group, index, me):
        size = self.sizes[group]
        if size <= PER_GROUP:
            each = PER_GROUP // size
            return None, me % size * each + index
        stride = size // PER_GROUP
        return me % stride == stride // 2 - 1, me % size // stride


def guarded(condition, body):
    if condition is None:
        body()
    else:
        pl.when(condition)(body)


def spread_matrix(offset, high):
    row = lax.broadcasted_iota(jnp.int32, (WINDOW, PER_GROUP * LANES), 0)
    col = lax.broadcasted_iota(jnp.int32, (WINDOW, PER_GROUP * LANES), 1)
    lane = (col & (LANES - 1)) - (HALF if high else 0)
    head = col >> 7
    hit = (lane >= 0) & (lane < HEAD_DIM) & (row == offset + HEAD_DIM * head + lane)
    return hit.astype(F32).astype(BF16)


def window_of(group):
    first = group * PER_GROUP * HEAD_DIM
    begin = first // LANES * LANES
    return begin, first - begin


def permutation(length):
    eighth = length // 8
    bits = eighth.bit_length() - 1
    row = lax.broadcasted_iota(jnp.int32, (length, length), 0)
    col = lax.broadcasted_iota(jnp.int32, (length, length), 1)
    block = row >> bits
    residue = ((block & 1) << 2) | (block & 2) | (block >> 2)
    return col == ((row & (eighth - 1)) << 3) + residue


def attend(units, outs, slot, scale):
    tile0 = units[slot, 0]
    tile1 = units[slot, 1]
    low = lax.broadcasted_iota(jnp.int32, tile0.shape, 1) < HALF
    zero = jnp.zeros_like(tile0)
    scores = dot_nt(jnp.where(low, tile0, zero), tile1) * scale
    top = jnp.max(scores, axis=-1, keepdims=True)
    weights = jnp.exp(scores - top)
    probs = weights * (1.0 / jnp.sum(weights, axis=-1, keepdims=True))
    probs_bf = probs.astype(BF16)
    head_out = dot_nn(probs_bf, tile1)
    grad = jnp.where(low, zero, tile0)
    delta = jnp.sum(grad.astype(F32) * head_out, axis=-1, keepdims=True)
    score_grads = (scale * probs * (dot_nt(grad, tile1) - delta)).astype(BF16)
    outs[slot, 0] = jnp.where(low, dot_nn(score_grads, tile1), head_out).astype(BF16)
    outs[slot, 1] = jnp.where(low, dot_tn(score_grads, tile0), dot_tn(probs_bf, tile0)).astype(BF16)


BITS = 4
CHUNK = 16
Y = BITS
FIRST_X, FIRST_Y, FIRST_Z = (1, Y, 2, 3), (Y, 1, 2, 3), (2, 3, 1, Y)


def chunk_orders(rows_each):
    pattern = (FIRST_Z, FIRST_X, FIRST_Y)
    chunks = []
    for which in range(4):
        for index in range(rows_each // CHUNK):
            order = pattern[index % 3]
            if which == 3 and order is FIRST_Z:
                order = FIRST_X
            chunks.append((which, index * CHUNK, order))
    return chunks


def chunk_shapes(rows_each, width):
    shapes = []
    for _, _, order in chunk_orders(rows_each):
        open_dims = {3, 2, 1, Y}
        for axis in order:
            open_dims.remove(axis)
            shapes.append((2,) * len(open_dims) + (CHUNK, width // 2))
    return shapes


class Reducer:
    def __init__(self, rows_each, data, core, final, recvs, core_sems, sems, final_sems):
        self.data, self.core, self.final, self.recvs = data, core, final, recvs
        self.core_sems, self.sems, self.final_sems = core_sems, sems, final_sems
        self.chunks = chunk_orders(rows_each)
        self.me = lax.axis_index("seq")
        self.dp = lax.axis_index("dp")
        self.bit = [self.me // 2**k % 2 for k in range(BITS)] + [self.dp]
        self.started = []
        self.current = {}

    def peer(self, axis):
        if axis == Y:
            return {"dp": 1 - self.dp}
        return {"seq": self.me + 2**axis - self.bit[axis] * 2 ** (axis + 1)}

    def view(self, fixed, which, rows):
        index = [fixed.get(3 - d, slice(None)) for d in range(BITS)]
        return tuple(index) + (which, fixed.get(Y, slice(None)), rows)

    def copy(self, source, target, sems, number, axis):
        copy = pltpu.make_async_remote_copy(
            source, target, sems.at[0, number], sems.at[1, number],
            device_id=self.peer(axis), device_id_type=MESH,
        )
        copy.start()
        self.started.append(copy)
        return copy

    def core_start(self, which):
        other = self.view({0: 1 - self.bit[0]}, which, slice(None))
        self.current["core", which] = self.copy(
            self.data.at[other], self.core.at[which], self.core_sems, which, 0
        )

    def core_add(self, which):
        self.current["core", which].wait_recv()
        mine = self.view({0: self.bit[0]}, which, slice(None))
        self.data[mine] = (
            self.data[mine].astype(F32) + self.core[which].astype(F32)
        ).astype(BF16)

    def fixed(self, order, stage):
        return {axis: self.bit[axis] for axis in (0,) + order[:stage]}

    def start(self, number, stage):
        which, row, order = self.chunks[number]
        rows = pl.ds(row, CHUNK)
        if stage == len(order):
            mine = self.view(self.fixed(order, stage), which, rows)
            self.current[number] = self.copy(
                self.data.at[mine], self.final.at[which, rows], self.final_sems, number, Y
            )
            return
        fixed = self.fixed(order, stage)
        fixed[order[stage]] = 1 - self.bit[order[stage]]
        slot = number * len(order) + stage
        self.current[number] = self.copy(
            self.data.at[self.view(fixed, which, rows)], self.recvs[slot], self.sems, slot,
            order[stage],
        )

    def add(self, number, stage):
        self.current[number].wait_recv()
        which, row, order = self.chunks[number]
        mine = self.view(self.fixed(order, stage + 1), which, pl.ds(row, CHUNK))
        got = self.recvs[number * len(order) + stage][...]
        self.data[mine] = (self.data[mine].astype(F32) + got.astype(F32)).astype(BF16)

    def numbers(self, which):
        return [n for n, chunk in enumerate(self.chunks) if chunk[0] == which]

    def advance(self, which, phase):
        if phase == 0:
            self.core_add(which)
        for number in self.numbers(which):
            if phase > 0:
                self.add(number, phase - 1)
            self.start(number, phase)

    def finish(self, out_ref):
        numbers = range(len(self.chunks))
        for number in numbers:
            self.current[number].wait_recv()
        own_at = self.view(dict(enumerate(self.bit)), slice(None), slice(None))
        own = self.data[own_at].astype(F32)
        other = self.final[...].astype(F32)
        half = out_ref.shape[2] // 2
        low = self.dp == 0
        out_ref[:, :, :half] = jnp.where(low, own, other)
        out_ref[:, :, half:] = jnp.where(low, other, own)
        for copy in self.started:
            copy.wait_send()


def layer_kernel(plan, rows_each, direct, *refs):
    (x_ref, mask_ref, *weight_hbm, g_ref) = refs[:7]
    result_ref, tgrad_ref, wgrad_ref = refs[7:10]
    staged = refs[10 : 10 + GROUPS]
    refs = refs[10 + GROUPS :]
    (units, outs, back, acc, send_sem, recv_sem, ret_send, ret_recv, weights, load_sem) = refs[:10]
    length, seq = plan.length, plan.seq
    scale = 1.0 / math.sqrt(HEAD_DIM)
    me = lax.axis_index("seq")

    loads = [
        pltpu.make_async_copy(weight_hbm[k], weights.at[k], load_sem.at[k]) for k in range(4)
    ]
    for load in loads:
        load.start()
    back[...] = jnp.zeros_like(back)
    barrier = pltpu.get_barrier_semaphore()
    for step in range(1, seq):
        pl.semaphore_signal(
            barrier, inc=1, device_id={"seq": lax.rem(me + step, seq)}, device_id_type=MESH
        )
    if direct:
        pl.semaphore_signal(
            barrier, inc=1, device_id={"dp": 1 - lax.axis_index("dp")}, device_id_type=MESH
        )

    perm = permutation(length)
    perm_f = perm.astype(F32)
    perm_bf = perm_f.astype(BF16)
    x = dot_nn(perm_bf, x_ref[...]).astype(BF16)
    g = dot_nn(perm_bf, g_ref[...]).astype(BF16)
    bias_row = jnp.where(mask_ref[...] == 1, 0.0, MASKED)
    bias = jnp.sum(jnp.where(perm, jnp.broadcast_to(bias_row, perm.shape), 0.0), axis=1, keepdims=True)
    loads[0].wait()
    queries = dot_nn(x, weights[0]).astype(BF16)
    loads[1].wait()
    keys = dot_nn(x, weights[1]).astype(BF16)
    loads[2].wait()
    values = dot_nn(x, weights[2]).astype(BF16)
    loads[3].wait()
    grads = dot_nt(g, weights[3]).astype(BF16)
    lane = lax.broadcasted_iota(jnp.int32, (length, PER_GROUP * LANES), 1) & (LANES - 1)
    spreads = {}
    for group in range(GROUPS):
        begin, offset = window_of(group)
        if offset not in spreads:
            spreads[offset] = (spread_matrix(offset, False), spread_matrix(offset, True))
    for group in reversed(range(GROUPS)):
        begin, offset = window_of(group)
        low, high = spreads[offset]
        cut = slice(begin, begin + WINDOW)
        tile0 = dot_nn(queries[:, cut], low) + dot_nn(grads[:, cut], high)
        tile1 = dot_nn(keys[:, cut], low) + dot_nn(values[:, cut], high)
        tile0 = jnp.where(lane == HEAD_DIM, 1.0, tile0).astype(BF16)
        tile1 = jnp.where(lane == HEAD_DIM, bias, tile1).astype(BF16)
        for head in range(PER_GROUP):
            first = plan.start(group, head)
            rows = slice(first, first + plan.rows[group])
            lanes = slice(head * LANES, (head + 1) * LANES)
            staged[group][head, 0] = tile0[rows, lanes]
            staged[group][head, 1] = tile1[rows, lanes]

    pl.semaphore_wait(barrier, seq - 1 + (1 if direct else 0))

    def out_copies(group):
        size = plan.sizes[group]
        base = me - me % size
        rows = plan.rows[group]
        row = pl.multiple_of(me % size * rows, rows)
        for head in range(PER_GROUP):
            owner, slot = plan.place(group, head, base)
            source = staged[group].at[head]
            target = units.at[slot, :, pl.ds(row, rows), :]
            remote = functools.partial(
                pltpu.make_async_remote_copy,
                source, target, send_sem.at[group, head], recv_sem.at[slot],
                device_id={"seq": owner}, device_id_type=MESH,
            )
            local = functools.partial(pltpu.make_async_copy, source, target, recv_sem.at[slot])
            yield owner, remote, local

    for group in reversed(range(GROUPS)):
        for owner, remote, local in out_copies(group):
            pl.when(owner != me)(lambda: remote().start())
            pl.when(owner == me)(lambda: local().start())

    def returns(slot, group, index, head):
        size = plan.sizes[group]
        base = me - me % size
        rows = plan.rows[group]
        first = pl.multiple_of(plan.start(group, head), plan.length // 8)
        for step in range(size):
            j = lax.rem(me + step, size)
            source = outs.at[slot, :, pl.ds(pl.multiple_of(j * rows, rows), rows), :]
            target = back.at[group, head, :, pl.ds(first, rows), :]
            if step == 0:
                yield None, pltpu.make_async_copy(source, target, ret_recv.at[group])
            else:
                yield step, pltpu.make_async_remote_copy(
                    source, target, ret_send.at[slot, step], ret_recv.at[group],
                    device_id={"seq": base + j}, device_id_type=MESH,
                )

    def start_all(slot, group, index, head):
        for _, copy in returns(slot, group, index, head):
            copy.start()

    def wait_sends(slot, group, index, head):
        for step, copy in returns(slot, group, index, head):
            if step is not None:
                copy.wait_send()

    order = list(range(plan.slots))
    for slot in order:
        entries = plan.groups_of_slot(slot)
        if not entries:
            continue
        owned = [(group, index) + plan.owned(group, index, me) for group, index in entries]
        conditions = [o[2] for o in owned if o[2] is not None]
        active = functools.reduce(jnp.logical_or, conditions) if conditions else None

        def work(slot=slot):
            pltpu.make_async_copy(units.at[slot], units.at[slot], recv_sem.at[slot]).wait()
            attend(units, outs, slot, scale)

        guarded(active, work)
        for group, index, condition, head in owned:
            guarded(condition, functools.partial(start_all, slot, group, index, head))

    for group in reversed(range(GROUPS)):
        for owner, remote, local in out_copies(group):
            pl.when(owner != me)(lambda: remote().wait_send())

    acc[...] = jnp.zeros_like(acc)
    for group in range(GROUPS):
        pltpu.make_async_copy(staged[group], staged[group], ret_recv.at[group]).wait()
        begin, offset = window_of(group)
        low, high = spreads[offset]
        for tile in range(2):
            packed = jnp.concatenate([back[group, head, tile] for head in range(PER_GROUP)], axis=1)
            acc[2 * tile, :, begin : begin + WINDOW] += dot_nt(packed, low)
            acc[2 * tile + 1, :, begin : begin + WINDOW] += dot_nt(packed, high)
    for slot in order:
        for group, index in plan.groups_of_slot(slot):
            condition, head = plan.owned(group, index, me)
            guarded(condition, functools.partial(wait_sends, slot, group, index, head))

    query_rows = acc[0].astype(BF16)
    attention = acc[1].astype(BF16)
    key_rows = acc[2].astype(BF16)
    value_rows = acc[3].astype(BF16)
    pairs = [(x, query_rows), (x, key_rows), (x, value_rows), (attention, g)]

    def products():
        result = dot_nn(attention, weights[3]).astype(BF16)
        result_ref[...] = dot_tn(perm_bf, result).astype(BF16)
        token = (
            dot_nt(query_rows, weights[0])
            + dot_nt(key_rows, weights[1])
            + dot_nt(value_rows, weights[2])
        ).astype(BF16)
        tgrad_ref[...] = dot_tn(perm_bf, token).astype(BF16)

    if not direct:
        for which, (left, right) in enumerate(pairs):
            product = dot_tn(left, right)
            for target in range(seq):
                wgrad_ref[target, which] = product[target * rows_each : (target + 1) * rows_each]
        products()
        return

    data, core, final, core_sems, sems, final_sems, *recvs = refs[10:]
    reducer = Reducer(rows_each, data, core, final, recvs, core_sems, sems, final_sems)
    half = x_ref.shape[1] // 2

    for which, (left, right) in enumerate(pairs):
        product = dot_tn(left, right).astype(BF16)
        for target in range(seq):
            bits = tuple(target >> k & 1 for k in (3, 2, 1, 0))
            rows = product[target * rows_each : (target + 1) * rows_each]
            data[bits + (which, 0)] = rows[:, :half]
            data[bits + (which, 1)] = rows[:, half:]
        reducer.core_start(which)
        if which == 2:
            reducer.advance(0, 0)
    products()
    for step in range(1, 4 + BITS):
        for which in range(4):
            if 0 <= step - which <= BITS:
                reducer.advance(which, step - which)
    reducer.finish(wgrad_ref)


def run_layer(seq, x, mask, wq, wk, wv, wo, g, direct):
    length, width = x.shape
    plan = Plan(seq, length)
    rows_each = width // seq
    vmem = pl.BlockSpec(memory_space=pltpu.VMEM)
    hbm = pl.BlockSpec(memory_space=pl.ANY)
    if direct:
        grads_shape = (4, rows_each, width)
        shapes = chunk_shapes(rows_each, width)
        chunks = len(chunk_orders(rows_each))
        extra = [
            pltpu.VMEM((2,) * BITS + (4, 2, rows_each, width // 2), BF16),
            pltpu.VMEM((4, 2, 2, 2, 2, rows_each, width // 2), BF16),
            pltpu.VMEM((4, rows_each, width // 2), BF16),
            pltpu.SemaphoreType.DMA((2, 4)),
            pltpu.SemaphoreType.DMA((2, len(shapes))),
            pltpu.SemaphoreType.DMA((2, chunks)),
        ] + [pltpu.VMEM(shape, BF16) for shape in shapes]
    else:
        grads_shape = (seq, 4, rows_each, width)
        extra = []
    return pl.pallas_call(
        functools.partial(layer_kernel, plan, rows_each, direct),
        out_shape=(
            jax.ShapeDtypeStruct((length, width), BF16),
            jax.ShapeDtypeStruct((length, width), BF16),
            jax.ShapeDtypeStruct(grads_shape, F32),
        ),
        in_specs=[vmem] * 2 + [hbm] * 4 + [vmem],
        out_specs=[vmem] * 3,
        scratch_shapes=[
            pltpu.VMEM((PER_GROUP, 2, plan.rows[group], LANES), BF16) for group in range(GROUPS)
        ]
        + [
            pltpu.VMEM((plan.slots, 2, plan.unit_rows, LANES), BF16),
            pltpu.VMEM((plan.slots, 2, plan.unit_rows, LANES), BF16),
            pltpu.VMEM((GROUPS, PER_GROUP, 2, length, LANES), BF16),
            pltpu.VMEM((4, length, width), F32),
            pltpu.SemaphoreType.DMA((GROUPS, PER_GROUP)),
            pltpu.SemaphoreType.DMA((plan.slots,)),
            pltpu.SemaphoreType.DMA((plan.slots, seq)),
            pltpu.SemaphoreType.DMA((GROUPS,)),
            pltpu.VMEM((4, width, width), BF16),
            pltpu.SemaphoreType.DMA((4,)),
        ]
        + extra,
        compiler_params=pltpu.CompilerParams(
            collective_id=0, has_side_effects=True, vmem_limit_bytes=60 * 2**20
        ),
        name="layer",
    )(x, mask, wq, wk, wv, wo, g)


def per_device(tokens, valid_mask, w_query, w_key, w_value, w_out, result_grad):
    seq, dp = lax.axis_size("seq"), lax.axis_size("dp")
    width = tokens.shape[2]
    rows_each = width // seq
    direct = seq == 2**BITS and dp == 2 and rows_each % CHUNK == 0
    result, token_grads, parts = run_layer(
        seq, tokens[0], valid_mask, w_query, w_key, w_value, w_out, result_grad[0],
        direct,
    )
    if direct:
        weight_grads = parts
    else:
        content = parts.reshape(seq, dp, -1).transpose(1, 0, 2).reshape(-1)
        share = lax.psum_scatter(content, ("dp", "seq"), scatter_dimension=0, tiled=True)
        weight_grads = lax.all_gather(share, "dp", axis=0, tiled=True).reshape(4, rows_each, width)
    return (result[None], token_grads[None], weight_grads)


def solution(mesh):
    return jax.shard_map(
        per_device,
        mesh=mesh,
        in_specs=(P("dp", "seq", None), P("dp", "seq"), P(), P(), P(), P(), P("dp", "seq", None)),
        out_specs=(P("dp", "seq", None), P("dp", "seq", None), P(None, "seq", None)),
        check_vma=False,
    )
```
